32 devices in a mesh: dp: 4 (over y, x), expert: 8 (over z, core).
Axes of the slice: x: 2, y: 2, z: 4, core: 2. Of those that a mesh axis runs over, the one named last changes fastest.
Arguments:
- saved_input: bfloat16 [1024, 2048], P(('dp', 'expert')), may hold values from -6 to 6
- output_grad: bfloat16 [1024, 2048], P(('dp', 'expert')), may hold values from -6 to 6
- route_probs: float32 [1024, 8], P(('dp', 'expert')), may hold values from 0.02 to 0.4
- expert_choice: int32 [1024, 8], P(('dp', 'expert')), may hold values from 0 to 15, all different within a row; in each aligned block of 32 rows (0 to 31, 32 to 63, ...) at most 24 rows name the same one
- slot_expert: int32 [4, 8], replicated, may hold values from 0 to 15, as said below
- frozen_gate: bfloat16 [32, 2048, 768], P(('dp', 'expert')), as said below
- frozen_up: bfloat16 [32, 2048, 768], P(('dp', 'expert')), as said below
- frozen_down: bfloat16 [32, 768, 2048], P(('dp', 'expert')), as said below
- adapter_in: float32 [16, 64, 768], P('expert', 'dp'), may hold values from -0.21875 to 0.21875
- adapter_out: float32 [16, 64, 2048], P('expert', 'dp'), may hold values from -0.125 to 0.125
- moment_in: float32 [16, 64, 768], P('expert', 'dp'), may hold values from -3 to 3
- moment_out: float32 [16, 64, 2048], P('expert', 'dp'), may hold values from -3 to 3
- second_in: float32 [16, 64, 768], P('expert', 'dp'), may hold values from 0.01 to 1
- second_out: float32 [16, 64, 2048], P('expert', 'dp'), may hold values from 0.01 to 1
Outputs:
- input_grad: bfloat16 [1024, 2048], P(('dp', 'expert'))
- step_in: float32 [16, 64, 768], P('expert', 'dp')
- step_out: float32 [16, 64, 2048], P('expert', 'dp')
- momentum_in: float32 [16, 64, 768], P('expert', 'dp')
- momentum_out: float32 [16, 64, 2048], P('expert', 'dp')
- variance_in: float32 [16, 64, 768], P('expert', 'dp')
- variance_out: float32 [16, 64, 2048], P('expert', 'dp')
- replica_in: bfloat16 [32, 64, 768], P(('dp', 'expert'))
- replica_out: bfloat16 [32, 64, 2048], P(('dp', 'expert'))
The draws below stay inside these ranges and needn't reach their ends.
Inputs may be any that keep to these rules, and one draw needn't show every extreme that they name: `expert_choice`: among the rows of one device no expert is named more than 24 times. `slot_expert`: the slots of index j of the expert axis host only experts 2 * j to 2 * j + 1, and each of these at least once. `frozen_gate`: slots that host the same expert hold the same frozen weights. `frozen_up`: slots that host the same expert hold the same frozen weights. `frozen_down`: slots that host the same expert hold the same frozen weights.
All inputs are finite; a program needn't handle non-finite values.
Results may differ from the reference program's by a relative error of at most 0.012.
Values may be sent and summed in bfloat16 or wider, within the bound.
No kernel may reach another device: no remote copies, remote signals or barrier semaphores. Data moves between devices by JAX's collectives and lax.ppermute only.
A program may use at most 128 MiB of HBM per device.

```python
import math
import jax
import jax.numpy as jnp
import numpy as np
from jax import lax

D = 2048
H = 768
TOPK = 8
R = 64
EXP_COL = 2
STEP = 100
TOK_DEV = 32
EXPERTS = 16
SLOTS = 32
TOKENS = 1024
CAP = 24
N_DP = 4
N_EXPERT = 8


def slot_table(key):
    salted = jax.random.fold_in(key, 7)
    first_key, second_key = jax.random.split(salted)
    extra = jax.random.randint(first_key, (N_EXPERT, N_DP), 0, EXP_COL)
    places = jnp.arange(N_DP, dtype=jnp.int32)
    local = jnp.where(places[None, :] < EXP_COL, places[None, :], extra)
    column_keys = jax.random.split(second_key, N_EXPERT)
    shuffle = jax.vmap(lambda inner_key: jax.random.permutation(inner_key, N_DP))(column_keys)
    mixed = jnp.take_along_axis(local, shuffle, axis=1)
    hosting = mixed + EXP_COL * jnp.arange(N_EXPERT, dtype=jnp.int32)[:, None]
    return hosting.T.astype(jnp.int32)


def expert_weights(key, salt, height, breadth, fan_in):
    hosting = slot_table(key).reshape(-1)
    salted = jax.random.fold_in(key, salt)

    def per_slot(expert):
        values = jax.random.truncated_normal(jax.random.fold_in(salted, expert), -4.0, 4.0, (height, breadth), jnp.float32)
        return (values * fan_in ** (-0.5)).astype(jnp.bfloat16)
    return jax.lax.map(per_slot, hosting)


def draw_slot_expert(key, part):
    return slot_table(key)


def draw_frozen_gate(key, part):
    return expert_weights(key, 101, D, H, D)


def draw_frozen_up(key, part):
    return expert_weights(key, 202, D, H, D)


def draw_frozen_down(key, part):
    return expert_weights(key, 303, H, D, H)


def steps_of(stream_key, extent, cuts, low, largest):
    def one(dim, parts):
        heights = jax.random.uniform(jax.random.fold_in(jax.random.fold_in(stream_key, 6), dim), (parts,), jnp.float32, low / len(cuts), largest / len(cuts))
        return jnp.repeat(jnp.exp(heights), extent[dim] // parts).reshape((-1,) + (1,) * (len(extent) - dim - 1))

    level = one(*cuts[0])
    for cut in cuts[1:]:
        level = level * one(*cut)
    return level


def assign_block(rng, own, number, rows, number_of, top, reach, slope):
    sequence = jax.random.permutation(rng, number_of)
    crowded, usual = portions_of(number_of, rows * top, reach, slope, True), portions_of(number_of, rows * top, reach, slope, False)
    places = jnp.arange(number_of)

    def named(sizes, offset_by):
        used = int((sizes > 0).sum())
        fixed = max(1, used // 4)
        shifted = fixed + (places - fixed + offset_by * (used - fixed)) % max(1, number_of - fixed)
        return jnp.zeros((number_of,), jnp.int32).at[sequence[jnp.where(places < fixed, places, shifted)]].set(jnp.asarray(sizes, jnp.int32))

    sizes = jnp.where(number % 4 == 0, named(crowded, number // 4), named(usual, number - number // 4 - 1))
    mixed = jax.random.permutation(jax.random.fold_in(own, 3), number_of)
    source_of, taker = mixed[0:number_of // 2 * 2:2], mixed[1:number_of // 2 * 2:2]
    margin = jnp.minimum(sizes[source_of] - 1, reach - sizes[taker]) // 2
    margin = jnp.where((source_of == sequence[0]) | (taker == sequence[0]) | (sizes[taker] == 0), 0, jnp.maximum(margin, 0))
    shifted = jax.random.randint(jax.random.fold_in(own, 4), (number_of // 2,), 0, 1 << 20) % (margin + 1)
    sizes = sizes.at[source_of].add(-shifted).at[taker].add(shifted)
    members = jnp.searchsorted(jnp.cumsum(sizes), jnp.arange(rows * top), side="right").astype(jnp.int32)
    grid = members.reshape(top, rows).T
    grid = grid[jax.random.permutation(jax.random.fold_in(own, 1), rows)]
    offset_by = jax.random.randint(jax.random.fold_in(own, 2), (rows, 1), 0, top)
    return jnp.take_along_axis(grid, (jnp.arange(top)[None, :] + offset_by) % top, axis=1)


def portions_of(count, total, reach, lean, full):
    portions = [(1 << 20) // math.isqrt(standing ** lean) + 1 for standing in range(1, count + 1)]
    largest = reach if full else min(reach, max(-(-total // count), total * portions[0] // sum(portions)))
    least = 1 if total - largest >= count - 1 else 0
    given, surplus = [largest] + [least] * (count - 1), total - largest - least * (count - 1)
    while surplus > 0:
        candidates = [i for i in range(1, count) if given[i] < largest] or [i for i in range(1, count) if given[i] < reach]
        pool, remaining = sum([portions[i] for i in candidates]), surplus
        for i in candidates:
            more = min(reach - given[i], max(1, remaining * portions[i] // pool), surplus)
            given[i] = given[i] + more
            surplus = surplus - more
    return np.array(given)


def scatter_about(stream_key, dims, scale, limit, pieces=(), kind=jnp.bfloat16):
    loudness = steps_of(stream_key, dims, pieces, -0.22, 0.18) if pieces else 1.0
    array = jax.random.normal(stream_key, dims, jnp.float32) * scale * loudness
    return jnp.minimum(jnp.maximum(array, -limit), limit).astype(kind)


def setup_inputs(seed: int = 0) -> dict:
    streams_of = jax.random.split(jax.random.key(seed), 15)
    saved_input = scatter_about(streams_of[0], (TOKENS, D), 1.0, 6.0, ((0, 32),))
    output_grad = scatter_about(streams_of[1], (TOKENS, D), 1.0, 6.0, ((0, 32),))
    route_probs = jnp.clip(0.02 + 0.38 * jax.random.uniform(streams_of[2], (TOKENS, TOPK), jnp.float32) ** steps_of(streams_of[2], (TOKENS, TOPK), ((0, 32),), -0.2, 0.2), 0.02, 0.4)
    expert_choice_keys = jax.random.split(jax.random.fold_in(streams_of[3], 1), TOKENS // TOK_DEV)
    expert_choice_turns = jax.random.permutation(jax.random.fold_in(streams_of[3], 3), TOKENS // TOK_DEV)
    expert_choice = jax.vmap(lambda own, number: assign_block(jax.random.fold_in(streams_of[3], 2), own, number, TOK_DEV, EXPERTS, TOPK, CAP, 2))(expert_choice_keys, expert_choice_turns).reshape((TOKENS, TOPK))
    slot_expert = draw_slot_expert(jax.random.fold_in(streams_of[14], 71), 0)
    frozen_gate = draw_frozen_gate(jax.random.fold_in(streams_of[14], 71), 0)
    frozen_up = draw_frozen_up(jax.random.fold_in(streams_of[14], 71), 0)
    frozen_down = draw_frozen_down(jax.random.fold_in(streams_of[14], 71), 0)
    adapter_in = scatter_about(streams_of[8], (EXPERTS, R, H), H ** -0.5, 0.21875, ((0, 8), (1, 4)), jnp.float32)
    adapter_out = scatter_about(streams_of[9], (EXPERTS, R, D), D ** -0.5, 0.125, ((0, 8), (1, 4)), jnp.float32)
    moment_in = scatter_about(streams_of[10], (EXPERTS, R, H), 0.3, 3.0, ((0, 8), (1, 4)), jnp.float32)
    moment_out = scatter_about(streams_of[11], (EXPERTS, R, D), 0.3, 3.0, ((0, 8), (1, 4)), jnp.float32)
    second_in = jnp.clip(jnp.exp(math.log(1.0) - 4.6051702 * jax.random.uniform(streams_of[12], (EXPERTS, R, H), jnp.float32) ** steps_of(streams_of[12], (EXPERTS, R, H), ((0, 8), (1, 4)), -0.2, 0.2)), 0.01, 1.0)
    second_out = jnp.clip(jnp.exp(math.log(1.0) - 4.6051702 * jax.random.uniform(streams_of[13], (EXPERTS, R, D), jnp.float32) ** steps_of(streams_of[13], (EXPERTS, R, D), ((0, 8), (1, 4)), -0.2, 0.2)), 0.01, 1.0)
    return dict(saved_input=saved_input, output_grad=output_grad, route_probs=route_probs, expert_choice=expert_choice, slot_expert=slot_expert, frozen_gate=frozen_gate, frozen_up=frozen_up, frozen_down=frozen_down, adapter_in=adapter_in, adapter_out=adapter_out, moment_in=moment_in, moment_out=moment_out, second_in=second_in, second_out=second_out)


adapter_scale_factor = 2.0
beta_one = 0.9
beta_two = 0.999
decay_rate = 0.01
adam_eps = 1e-08

def route_all(expert_choice, slot_expert):
    row_count = TOKENS * TOPK
    flat = expert_choice.reshape(row_count).astype(jnp.int32)
    row_ids = jnp.arange(row_count, dtype=jnp.int32)
    source = row_ids // (TOK_DEV * TOPK)
    column = flat // EXP_COL
    hosted = (slot_expert[:, column] == flat[None, :]).astype(jnp.int32)
    counts = lax.optimization_barrier(jnp.sum(hosted, axis=0))
    picked = source % counts
    running = jnp.cumsum(hosted, axis=0) - 1
    chosen = hosted * (running == picked[None, :]).astype(jnp.int32)
    dest_row = lax.optimization_barrier(jnp.sum(chosen * jnp.arange(N_DP, dtype=jnp.int32)[:, None], axis=0))
    blocks = flat.reshape(SLOTS, TOK_DEV * TOPK)
    inner = jnp.arange(TOK_DEV * TOPK, dtype=jnp.int32)
    earlier = (blocks[:, None, :] == blocks[:, :, None]) & (inner[None, None, :] < inner[None, :, None])
    rank = lax.optimization_barrier(jnp.sum(earlier.astype(jnp.int32), axis=2)).reshape(row_count)
    slot = dest_row * N_EXPERT + column
    return (slot * SLOTS + source) * CAP + rank

def expert_backward(buffer_rows, gradient_row_block, gate_weight, up_weight, down_weight, owned_input, own_out):
    gate_pre = jnp.dot(buffer_rows, gate_weight, preferred_element_type=jnp.float32)
    up_pre = jnp.dot(buffer_rows, up_weight, preferred_element_type=jnp.float32)
    sigmoid_gate = jax.nn.sigmoid(gate_pre)
    hidden_state = (gate_pre * sigmoid_gate * up_pre).astype(jnp.bfloat16)
    low_rank_input = jnp.dot(hidden_state, owned_input.T, preferred_element_type=jnp.float32).astype(jnp.bfloat16)
    low_rank_gradient = jnp.dot(gradient_row_block, own_out.T, preferred_element_type=jnp.float32).astype(jnp.bfloat16)
    hidden_gradient = jnp.dot(gradient_row_block, down_weight.T, preferred_element_type=jnp.float32)
    hidden_gradient = hidden_gradient + adapter_scale_factor * jnp.dot(low_rank_gradient, owned_input, preferred_element_type=jnp.float32)
    up_grad = (hidden_gradient * gate_pre * sigmoid_gate).astype(jnp.bfloat16)
    gate_grad = (hidden_gradient * up_pre * sigmoid_gate * (1.0 + gate_pre * (1.0 - sigmoid_gate))).astype(jnp.bfloat16)
    back_rows = jnp.dot(gate_grad, gate_weight.T, preferred_element_type=jnp.float32)
    back_rows = (back_rows + jnp.dot(up_grad, up_weight.T, preferred_element_type=jnp.float32)).astype(jnp.bfloat16)
    incoming_gradient = adapter_scale_factor * jnp.dot(low_rank_gradient.T, hidden_state, preferred_element_type=jnp.float32)
    outgoing_gradient = adapter_scale_factor * jnp.dot(low_rank_input.T, gradient_row_block, preferred_element_type=jnp.float32)
    return (back_rows, incoming_gradient, outgoing_gradient)

def adamw(param, grad, first, second):
    first_new = beta_one * first + (1.0 - beta_one) * grad
    second_new = beta_two * second + (1.0 - beta_two) * grad * grad
    corr_one = 1.0 - beta_one ** STEP
    corr_two = 1.0 - beta_two ** STEP
    step_dir = first_new / corr_one / (jnp.sqrt(second_new / corr_two) + adam_eps) + decay_rate * param
    return (step_dir, first_new, second_new)

def reference(saved_input, output_grad, route_probs, expert_choice, slot_expert, frozen_gate, frozen_up, frozen_down, adapter_in, adapter_out, moment_in, moment_out, second_in, second_out):
    row_count = TOKENS * TOPK
    position = route_all(expert_choice, slot_expert)
    row_ids = jnp.arange(row_count, dtype=jnp.int32)
    block_rows = SLOTS * CAP
    filler = jnp.full((SLOTS * block_rows,), row_count, jnp.int32).at[position].set(row_ids)
    scaled = (route_probs[:, :, None] * output_grad[:, None, :].astype(jnp.float32)).astype(jnp.bfloat16).reshape(row_count, D)
    hosting = slot_expert.reshape(SLOTS).astype(jnp.int32)

    def one_slot(carry, slot):
        grad_acc, sum_in, sum_out = carry
        picked = lax.dynamic_slice_in_dim(filler, slot * block_rows, block_rows)
        token_idx = picked // TOPK
        buffer_rows = jnp.take(saved_input, token_idx, axis=0, mode='fill', fill_value=0)
        gradient_row_block = jnp.take(scaled, picked, axis=0, mode='fill', fill_value=0)
        expert = hosting[slot]
        owned_input = adapter_in[expert].astype(jnp.bfloat16)
        own_out = adapter_out[expert].astype(jnp.bfloat16)
        back_rows, incoming_gradient, outgoing_gradient = expert_backward(buffer_rows, gradient_row_block, frozen_gate[slot], frozen_up[slot], frozen_down[slot], owned_input, own_out)
        grad_acc = grad_acc.at[token_idx].add(back_rows.astype(jnp.float32), mode='drop')
        sum_in = sum_in.at[expert].add(incoming_gradient)
        sum_out = sum_out.at[expert].add(outgoing_gradient)
        return ((grad_acc, sum_in, sum_out), None)
    start = (jnp.zeros((TOKENS, D), jnp.float32), jnp.zeros((EXPERTS, R, H), jnp.float32), jnp.zeros((EXPERTS, R, D), jnp.float32))
    (grad_acc, sum_in, sum_out), _ = lax.scan(one_slot, start, jnp.arange(SLOTS, dtype=jnp.int32))
    input_grad = grad_acc.astype(jnp.bfloat16)
    step_in, momentum_in, variance_in = adamw(adapter_in, sum_in, moment_in, second_in)
    step_out, momentum_out, variance_out = adamw(adapter_out, sum_out, moment_out, second_out)
    replica_in = step_in.astype(jnp.bfloat16)[hosting]
    replica_out = step_out.astype(jnp.bfloat16)[hosting]
    return (input_grad, step_in, step_out, momentum_in, momentum_out, variance_in, variance_out, replica_in, replica_out)
```

```python
import jax
import jax.numpy as jnp
from jax import lax
from jax.sharding import PartitionSpec as P

STEP = 100


adapter_scale_factor = 2.0
beta_one = 0.9
beta_two = 0.999
decay_rate = 0.01
adam_eps = 1e-08


def contract_product(left, right, left_dim, right_dim):
    return lax.dot_general(
        left, right, (((left_dim,), (right_dim,)), ((), ())), preferred_element_type=jnp.float32
    )


def route_rows(choice_flat, slot_expert, source, local_experts):
    column = choice_flat // local_experts
    hosted = (jnp.take(slot_expert, column, axis=1) == choice_flat[None, :]).astype(jnp.int32)
    counts = jnp.sum(hosted, axis=0)
    picked = source % counts
    running = jnp.cumsum(hosted, axis=0) - 1
    chosen = hosted * (running == picked[None, :]).astype(jnp.int32)
    dp_ids = jnp.arange(hosted.shape[0], dtype=jnp.int32)
    dest_row = jnp.sum(chosen * dp_ids[:, None], axis=0)
    row_ids = jnp.arange(choice_flat.shape[0], dtype=jnp.int32)
    earlier = (choice_flat[None, :] == choice_flat[:, None]) & (row_ids[None, :] < row_ids[:, None])
    rank = jnp.sum(earlier.astype(jnp.int32), axis=1)
    return (dest_row, column, rank)


def pack_rows(saved_input, scaled, position, buffer_size, top_count, shape_out):
    row_count = scaled.shape[0]
    row_ids = jnp.arange(row_count, dtype=jnp.int32)
    filler = jnp.full((buffer_size,), row_count, jnp.int32).at[position].set(row_ids)
    send_input = jnp.take(saved_input, filler // top_count, axis=0, mode="fill", fill_value=0)
    send_grad = jnp.take(scaled, filler, axis=0, mode="fill", fill_value=0)
    return (send_input.reshape(shape_out), send_grad.reshape(shape_out))


def adamw(param, grad, first, second):
    first_new = beta_one * first + (1.0 - beta_one) * grad
    second_new = beta_two * second + (1.0 - beta_two) * grad * grad
    corr_one = 1.0 - beta_one**STEP
    corr_two = 1.0 - beta_two**STEP
    step_dir = (
        first_new / corr_one / (jnp.sqrt(second_new / corr_two) + adam_eps) + decay_rate * param
    )
    return (step_dir, first_new, second_new)


def packed_device(
    saved_input,
    output_grad,
    route_probs,
    expert_choice,
    slot_expert,
    frozen_gate,
    frozen_up,
    frozen_down,
    adapter_in,
    adapter_out,
    moment_in,
    moment_out,
    second_in,
    second_out,
):
    dp_count = lax.axis_size("dp")
    expert_count = lax.axis_size("expert")
    dp_index = lax.axis_index("dp")
    column_index = lax.axis_index("expert")
    local_experts = adapter_in.shape[0]
    token_count, top_count = expert_choice.shape
    width = saved_input.shape[1]
    row_count = token_count * top_count
    capacity = max(2, -(-3 * row_count // (2 * local_experts * expert_count)))
    buffer_size = dp_count * expert_count * capacity
    source = dp_index * expert_count + column_index
    choice_flat = expert_choice.reshape(row_count)
    dest_row, column, rank = route_rows(choice_flat, slot_expert, source, local_experts)
    scaled = (
        (route_probs[:, :, None] * output_grad[:, None, :].astype(jnp.float32))
        .astype(jnp.bfloat16)
        .reshape(row_count, width)
    )
    col_size = local_experts * expert_count * capacity
    col_position = (choice_flat % local_experts * expert_count + column) * capacity + rank
    col_shape = (local_experts, expert_count, capacity, width)
    col_input, col_grad = pack_rows(
        saved_input, scaled, col_position, col_size, top_count, col_shape
    )
    got_input, got_grad = (
        lax.all_to_all(col_input, "expert", split_axis=1, concat_axis=1, tiled=True),
        lax.all_to_all(col_grad, "expert", split_axis=1, concat_axis=1, tiled=True),
    )
    column_hosts = lax.dynamic_index_in_dim(slot_expert, column_index, 1, keepdims=False)
    dp_ids = jnp.arange(dp_count, dtype=jnp.int32)
    same_host = (column_hosts[:, None] == column_hosts[None, :]).astype(jnp.int32)
    host_count = jnp.sum(same_host, axis=1)
    host_place = jnp.sum(same_host * (dp_ids[None, :] < dp_ids[:, None]).astype(jnp.int32), axis=1)
    sources = dp_index * expert_count + jnp.arange(expert_count, dtype=jnp.int32)
    serves = sources[None, :] % host_count[:, None] == host_place[:, None]
    local_of = column_hosts - local_experts * column_index
    kept_mask = serves[:, :, None, None]
    zero_value = jnp.zeros((), jnp.bfloat16)
    picked_input = jnp.where(kept_mask, jnp.take(got_input, local_of, axis=0), zero_value)
    picked_grad = jnp.where(kept_mask, jnp.take(got_grad, local_of, axis=0), zero_value)
    arrived_input, arrived_grad = (
        lax.all_to_all(picked_input, "dp", split_axis=0, concat_axis=0, tiled=True),
        lax.all_to_all(picked_grad, "dp", split_axis=0, concat_axis=0, tiled=True),
    )
    fetched_in, fetched_out = (
        lax.all_gather(adapter_in.astype(jnp.bfloat16), "dp", axis=1, tiled=True),
        lax.all_gather(adapter_out.astype(jnp.bfloat16), "dp", axis=1, tiled=True),
    )
    hosted_local = slot_expert[dp_index, column_index] - local_experts * column_index
    owned_input = lax.dynamic_index_in_dim(fetched_in, hosted_local, 0, keepdims=False)
    own_out = lax.dynamic_index_in_dim(fetched_out, hosted_local, 0, keepdims=False)
    buffer_rows = arrived_input.reshape(buffer_size, width)
    gradient_row_block = arrived_grad.reshape(buffer_size, width)
    gate_weight = frozen_gate[0]
    up_weight = frozen_up[0]
    down_weight = frozen_down[0]
    gate_pre = jnp.dot(buffer_rows, gate_weight, preferred_element_type=jnp.float32)
    up_pre = jnp.dot(buffer_rows, up_weight, preferred_element_type=jnp.float32)
    sigmoid_gate = jax.nn.sigmoid(gate_pre)
    hidden_state = (gate_pre * sigmoid_gate * up_pre).astype(jnp.bfloat16)
    low_rank_input = contract_product(hidden_state, owned_input, 1, 1).astype(jnp.bfloat16)
    low_rank_gradient = contract_product(gradient_row_block, own_out, 1, 1).astype(jnp.bfloat16)
    hidden_gradient = contract_product(gradient_row_block, down_weight, 1, 1)
    hidden_gradient = hidden_gradient + adapter_scale_factor * jnp.dot(
        low_rank_gradient, owned_input, preferred_element_type=jnp.float32
    )
    up_grad = (hidden_gradient * gate_pre * sigmoid_gate).astype(jnp.bfloat16)
    gate_grad = (
        hidden_gradient * up_pre * sigmoid_gate * (1.0 + gate_pre * (1.0 - sigmoid_gate))
    ).astype(jnp.bfloat16)
    back_rows = (
        contract_product(gate_grad, gate_weight, 1, 1) + contract_product(up_grad, up_weight, 1, 1)
    ).astype(jnp.bfloat16)
    incoming_gradient = adapter_scale_factor * contract_product(
        low_rank_gradient, hidden_state, 0, 0
    )
    outgoing_gradient = adapter_scale_factor * contract_product(
        low_rank_input, gradient_row_block, 0, 0
    )
    back_block = back_rows.reshape(dp_count, expert_count, capacity, width)
    came_back = lax.all_to_all(back_block, "dp", split_axis=0, concat_axis=0, tiled=True)
    pieces_back = []
    for which_local in range(local_experts):
        chosen_mask = (serves & (local_of == which_local)[:, None])[:, :, None, None]
        pieces_back.append(jnp.sum(jnp.where(chosen_mask, came_back, zero_value), axis=0))
    gone_back = lax.all_to_all(
        jnp.stack(pieces_back), "expert", split_axis=1, concat_axis=1, tiled=True
    )
    per_row = jnp.take(gone_back.reshape(col_size, width), col_position, axis=0)
    input_grad = jnp.sum(
        per_row.reshape(token_count, top_count, width).astype(jnp.float32), axis=1
    ).astype(jnp.bfloat16)
    selector = (jnp.arange(local_experts, dtype=jnp.int32) == hosted_local).astype(jnp.float32)
    placed_in = selector[:, None, None] * incoming_gradient[None, :, :]
    placed_out = selector[:, None, None] * outgoing_gradient[None, :, :]
    summed_in, summed_out = (
        lax.psum_scatter(placed_in, "dp", scatter_dimension=1, tiled=True),
        lax.psum_scatter(placed_out, "dp", scatter_dimension=1, tiled=True),
    )
    step_in, momentum_in, variance_in = adamw(adapter_in, summed_in, moment_in, second_in)
    step_out, momentum_out, variance_out = adamw(adapter_out, summed_out, moment_out, second_out)
    copied_in, copied_out = (
        lax.all_gather(step_in.astype(jnp.bfloat16), "dp", axis=1, tiled=True),
        lax.all_gather(step_out.astype(jnp.bfloat16), "dp", axis=1, tiled=True),
    )
    replica_in = lax.dynamic_index_in_dim(copied_in, hosted_local, 0, keepdims=True)
    replica_out = lax.dynamic_index_in_dim(copied_out, hosted_local, 0, keepdims=True)
    return (
        input_grad,
        step_in,
        step_out,
        momentum_in,
        momentum_out,
        variance_in,
        variance_out,
        replica_in,
        replica_out,
    )


def flip_chip(array, distance, size):
    return lax.ppermute(array, "expert", [(i, i ^ (2 * distance)) for i in range(size)])


def flip_core(array, size):
    return lax.ppermute(array, "expert", [(i, i ^ 1) for i in range(size)])


def flip_plane(array, dp_count, size, masks):
    pairs = [
        (row * size + col, (row ^ masks[col % 2]) * size + col)
        for row in range(dp_count)
        for col in range(size)
    ]
    return lax.ppermute(array, ("dp", "expert"), pairs)


def add_rounded(left, right):
    return (left.astype(jnp.float32) + right.astype(jnp.float32)).astype(jnp.bfloat16)


def dense_probs(route_probs, expert_choice, expert_total):
    ids = jnp.arange(expert_total, dtype=jnp.int32)
    named = expert_choice[:, :, None] == ids[None, None, :]
    return jnp.sum(jnp.where(named, route_probs[:, :, None], 0.0), axis=1)


def split_three(value):
    high = lax.reduce_precision(value, 8, 7)
    rest = value - high
    middle = lax.reduce_precision(rest, 8, 7)
    low = rest - middle
    return [part.astype(jnp.bfloat16) for part in (high, middle, low)]


def host_tables(slot_expert, dp_count, column_index, dp_index, local_experts):
    hosts = lax.dynamic_index_in_dim(slot_expert, column_index, 1, keepdims=False)
    local_of = hosts - local_experts * column_index
    dp_ids = jnp.arange(dp_count, dtype=jnp.int32)
    mine = lax.dynamic_index_in_dim(hosts, dp_index, 0, keepdims=False)
    same = (hosts == mine).astype(jnp.int32)
    count = jnp.sum(same)
    place = jnp.sum(same * (dp_ids < dp_index).astype(jnp.int32))
    return (local_of, mine, count, place)


def pick_local(stacked, local_of):
    count = stacked.shape[0]
    total = jnp.zeros((local_of.shape[0],) + stacked.shape[1:], stacked.dtype)
    for which in range(count):
        chosen = (local_of == which).reshape((-1,) + (1,) * (stacked.ndim - 1))
        total = jnp.where(chosen, stacked[which][None], total)
    return total


def expert_rows(rows, gradient, gate_weight, up_weight, down_weight, owned_input, own_out):
    gate_pre = jnp.dot(rows, gate_weight, preferred_element_type=jnp.float32)
    up_pre = jnp.dot(rows, up_weight, preferred_element_type=jnp.float32)
    sigmoid_gate = jax.nn.sigmoid(gate_pre)
    hidden_state = (gate_pre * sigmoid_gate * up_pre).astype(jnp.bfloat16)
    low_rank_input = contract_product(hidden_state, owned_input, 1, 1).astype(jnp.bfloat16)
    low_rank_gradient = contract_product(gradient, own_out, 1, 1).astype(jnp.bfloat16)
    hidden_gradient = contract_product(gradient, down_weight, 1, 1)
    hidden_gradient = hidden_gradient + adapter_scale_factor * jnp.dot(
        low_rank_gradient, owned_input, preferred_element_type=jnp.float32
    )
    up_grad = (hidden_gradient * gate_pre * sigmoid_gate).astype(jnp.bfloat16)
    gate_grad = (
        hidden_gradient * up_pre * sigmoid_gate * (1.0 + gate_pre * (1.0 - sigmoid_gate))
    ).astype(jnp.bfloat16)
    back_rows = (
        contract_product(gate_grad, gate_weight, 1, 1) + contract_product(up_grad, up_weight, 1, 1)
    ).astype(jnp.bfloat16)
    incoming = adapter_scale_factor * contract_product(low_rank_gradient, hidden_state, 0, 0)
    outgoing = adapter_scale_factor * contract_product(low_rank_input, gradient, 0, 0)
    return (back_rows, incoming, outgoing)


def dense_device(
    saved_input,
    output_grad,
    route_probs,
    expert_choice,
    slot_expert,
    frozen_gate,
    frozen_up,
    frozen_down,
    adapter_in,
    adapter_out,
    moment_in,
    moment_out,
    second_in,
    second_out,
):
    dp_count = lax.axis_size("dp")
    expert_count = lax.axis_size("expert")
    dp_index = lax.axis_index("dp")
    column_index = lax.axis_index("expert")
    local_experts = adapter_in.shape[0]
    tokens, top_count = expert_choice.shape
    width = saved_input.shape[1]
    hidden = adapter_in.shape[2]
    expert_total = local_experts * expert_count
    chips = expert_count // 2
    core = column_index % 2
    bf16 = jnp.bfloat16

    parts = split_three(dense_probs(route_probs, expert_choice, expert_total))
    spare = -(-3 * expert_total // 128) * 128 - 3 * expert_total
    block = jnp.concatenate(
        [saved_input, output_grad, *parts, jnp.zeros((tokens, spare), bf16)], axis=1
    )
    gathered = [block] + [flip_chip(block, z, expert_count) for z in range(1, chips)]
    mine_column = jnp.concatenate(gathered, axis=0)

    local_of, hosted, host_count, host_place = host_tables(
        slot_expert, dp_count, column_index, dp_index, local_experts
    )
    adapters = jnp.concatenate([adapter_in, adapter_out], axis=2).astype(bf16)
    fetched = lax.all_to_all(
        pick_local(adapters, local_of), "dp", split_axis=0, concat_axis=0, tiled=True
    )
    rank = dp_count * adapter_in.shape[1]
    fetched = fetched.reshape(rank, hidden + width)
    owned_input = fetched[:, :hidden]
    own_out = fetched[:, hidden:]

    other_column = flip_core(mine_column, expert_count)
    own_chunk = jnp.concatenate([mine_column, other_column], axis=0)
    side_chunk = flip_plane(own_chunk, dp_count, expert_count, (1, 2))
    half = chips * tokens
    far_mine = flip_plane(side_chunk[:half], dp_count, expert_count, (2, 1))
    cross_chunk = flip_core(side_chunk, expert_count)
    far_other = flip_core(far_mine, expert_count)
    arrived = jnp.concatenate([own_chunk, side_chunk, cross_chunk, far_mine, far_other], axis=0)

    near, far = jnp.where(core == 0, 1, 2), jnp.where(core == 0, 2, 1)
    chip_ids = jnp.arange(chips, dtype=jnp.int32)
    chip_index = column_index // 2

    def sources(row, col_core):
        return row * expert_count + (chip_index ^ chip_ids) * 2 + col_core

    ordered = jnp.concatenate(
        [
            sources(dp_index, core),
            sources(dp_index, 1 - core),
            sources(dp_index ^ near, core),
            sources(dp_index ^ near, 1 - core),
            sources(dp_index ^ far, 1 - core),
            sources(dp_index ^ far, core),
            sources(dp_index ^ 3, core),
            sources(dp_index ^ 3, 1 - core),
        ]
    )
    served = jnp.repeat(ordered % host_count == host_place, tokens)
    ids = jnp.arange(3 * expert_total, dtype=jnp.int32) % expert_total
    coded = arrived[:, 2 * width : 2 * width + 3 * expert_total].astype(jnp.float32)
    prob = jnp.sum(jnp.where((ids == hosted)[None, :] & served[:, None], coded, 0.0), axis=1)
    rows = jnp.where((prob != 0)[:, None], arrived[:, :width], jnp.zeros((), bf16))
    gradient = (prob[:, None] * arrived[:, width : 2 * width].astype(jnp.float32)).astype(bf16)
    back, incoming, outgoing = expert_rows(
        rows, gradient, frozen_gate[0], frozen_up[0], frozen_down[0], owned_input, own_out
    )
    block_rows = 2 * half
    own_back = back[:block_rows]
    side_back = back[block_rows : 2 * block_rows]
    cross_back = back[2 * block_rows : 3 * block_rows]
    far_back = back[3 * block_rows :]

    far_sum = add_rounded(far_back[:half], flip_core(far_back[half:], expert_count))
    far_got = flip_plane(far_sum, dp_count, expert_count, (2, 1))
    side_sum = side_back.astype(jnp.float32) + flip_core(cross_back, expert_count).astype(
        jnp.float32
    )
    late = (side_sum[:half] + far_got.astype(jnp.float32)).astype(bf16)
    early = side_sum[half:].astype(bf16)
    early_got = flip_plane(early, dp_count, expert_count, (1, 2))
    late_got = flip_plane(late, dp_count, expert_count, (1, 2))
    mine_sum = own_back[:half].astype(jnp.float32) + late_got.astype(jnp.float32)
    other_sum = add_rounded(own_back[half:], early_got)
    mine_sum = mine_sum + flip_core(other_sum, expert_count).astype(jnp.float32)
    pieces = mine_sum.reshape(chips, tokens, width)
    total = pieces[0]
    for z in range(1, chips):
        total = total + flip_chip(pieces[z].astype(bf16), z, expert_count).astype(jnp.float32)
    input_grad = total.astype(bf16)

    slot_grad = jnp.concatenate([incoming, outgoing], axis=1).astype(bf16)
    shares = lax.all_to_all(
        slot_grad.reshape(dp_count, rank // dp_count, hidden + width),
        "dp",
        split_axis=0,
        concat_axis=0,
        tiled=True,
    ).astype(jnp.float32)
    summed = jnp.stack(
        [
            jnp.sum(jnp.where((local_of == which)[:, None, None], shares, 0.0), axis=0)
            for which in range(local_experts)
        ]
    )
    step_in, momentum_in, variance_in = adamw(
        adapter_in, summed[:, :, :hidden], moment_in, second_in
    )
    step_out, momentum_out, variance_out = adamw(
        adapter_out, summed[:, :, hidden:], moment_out, second_out
    )
    steps = jnp.concatenate([step_in, step_out], axis=2).astype(bf16)
    copied = lax.all_to_all(
        pick_local(steps, local_of), "dp", split_axis=0, concat_axis=0, tiled=True
    ).reshape(1, rank, hidden + width)
    return (
        input_grad,
        step_in,
        step_out,
        momentum_in,
        momentum_out,
        variance_in,
        variance_out,
        copied[:, :, :hidden],
        copied[:, :, hidden:],
    )


def per_device(saved_input, output_grad, route_probs, expert_choice, *rest):
    dp_count = lax.axis_size("dp")
    expert_count = lax.axis_size("expert")
    tokens, top_count = expert_choice.shape
    local_experts = rest[4].shape[0]
    devices = dp_count * expert_count
    capacity = max(2, -(-3 * tokens * top_count // (2 * local_experts * expert_count)))
    whole = dp_count == 4 and expert_count >= 4 and expert_count & (expert_count - 1) == 0
    if whole and tokens <= 2 * capacity:
        return dense_device(saved_input, output_grad, route_probs, expert_choice, *rest)
    return packed_device(saved_input, output_grad, route_probs, expert_choice, *rest)


def solution(mesh):
    return jax.shard_map(
        per_device,
        mesh=mesh,
        in_specs=(
            P(("dp", "expert"), None),
            P(("dp", "expert"), None),
            P(("dp", "expert"), None),
            P(("dp", "expert"), None),
            P(),
            P(("dp", "expert"), None, None),
            P(("dp", "expert"), None, None),
            P(("dp", "expert"), None, None),
            P("expert", "dp", None),
            P("expert", "dp", None),
            P("expert", "dp", None),
            P("expert", "dp", None),
            P("expert", "dp", None),
            P("expert", "dp", None),
        ),
        out_specs=(
            P(("dp", "expert"), None),
            P("expert", "dp", None),
            P("expert", "dp", None),
            P("expert", "dp", None),
            P("expert", "dp", None),
            P("expert", "dp", None),
            P("expert", "dp", None),
            P(("dp", "expert"), None, None),
            P(("dp", "expert"), None, None),
        ),
        check_vma=False,
    )
```

```python
import functools

import jax
import jax.numpy as jnp
from jax import lax
from jax.experimental import pallas as pl
from jax.experimental.pallas import tpu as pltpu
from jax.sharding import PartitionSpec as P

STEP = 100


adapter_scale_factor = 2.0
beta_one = 0.9
beta_two = 0.999
decay_rate = 0.01
adam_eps = 1e-08
VMEM_LIMIT = 32 * 1024 * 1024


def contract_product(left, right, left_dim, right_dim):
    return lax.dot_general(
        left, right, (((left_dim,), (right_dim,)), ((), ())), preferred_element_type=jnp.float32
    )


def route_rows(choice_flat, slot_expert, source, local_experts):
    column = choice_flat // local_experts
    hosted = (jnp.take(slot_expert, column, axis=1) == choice_flat[None, :]).astype(jnp.int32)
    counts = jnp.sum(hosted, axis=0)
    picked = source % counts
    running = jnp.cumsum(hosted, axis=0) - 1
    chosen = hosted * (running == picked[None, :]).astype(jnp.int32)
    dp_ids = jnp.arange(hosted.shape[0], dtype=jnp.int32)
    dest_row = jnp.sum(chosen * dp_ids[:, None], axis=0)
    row_ids = jnp.arange(choice_flat.shape[0], dtype=jnp.int32)
    earlier = (choice_flat[None, :] == choice_flat[:, None]) & (row_ids[None, :] < row_ids[:, None])
    rank = jnp.sum(earlier.astype(jnp.int32), axis=1)
    return (dest_row, column, rank)


def pack_rows(saved_input, scaled, position, buffer_size, top_count, shape_out):
    row_count = scaled.shape[0]
    row_ids = jnp.arange(row_count, dtype=jnp.int32)
    filler = jnp.full((buffer_size,), row_count, jnp.int32).at[position].set(row_ids)
    send_input = jnp.take(saved_input, filler // top_count, axis=0, mode="fill", fill_value=0)
    send_grad = jnp.take(scaled, filler, axis=0, mode="fill", fill_value=0)
    return (send_input.reshape(shape_out), send_grad.reshape(shape_out))


def adamw(param, grad, first, second):
    first_new = beta_one * first + (1.0 - beta_one) * grad
    second_new = beta_two * second + (1.0 - beta_two) * grad * grad
    corr_one = 1.0 - beta_one**STEP
    corr_two = 1.0 - beta_two**STEP
    step_dir = (
        first_new / corr_one / (jnp.sqrt(second_new / corr_two) + adam_eps) + decay_rate * param
    )
    return (step_dir, first_new, second_new)


def packed_device(
    saved_input,
    output_grad,
    route_probs,
    expert_choice,
    slot_expert,
    frozen_gate,
    frozen_up,
    frozen_down,
    adapter_in,
    adapter_out,
    moment_in,
    moment_out,
    second_in,
    second_out,
):
    dp_count = lax.axis_size("dp")
    expert_count = lax.axis_size("expert")
    dp_index = lax.axis_index("dp")
    column_index = lax.axis_index("expert")
    local_experts = adapter_in.shape[0]
    token_count, top_count = expert_choice.shape
    width = saved_input.shape[1]
    row_count = token_count * top_count
    capacity = max(2, -(-3 * row_count // (2 * local_experts * expert_count)))
    buffer_size = dp_count * expert_count * capacity
    source = dp_index * expert_count + column_index
    choice_flat = expert_choice.reshape(row_count)
    _, column, rank = route_rows(choice_flat, slot_expert, source, local_experts)
    scaled = (
        (route_probs[:, :, None] * output_grad[:, None, :].astype(jnp.float32))
        .astype(jnp.bfloat16)
        .reshape(row_count, width)
    )
    col_size = local_experts * expert_count * capacity
    col_position = (choice_flat % local_experts * expert_count + column) * capacity + rank
    col_shape = (local_experts, expert_count, capacity, width)
    col_input, col_grad = pack_rows(
        saved_input, scaled, col_position, col_size, top_count, col_shape
    )
    got_input, got_grad = (
        lax.all_to_all(col_input, "expert", split_axis=1, concat_axis=1, tiled=True),
        lax.all_to_all(col_grad, "expert", split_axis=1, concat_axis=1, tiled=True),
    )
    column_hosts = lax.dynamic_index_in_dim(slot_expert, column_index, 1, keepdims=False)
    dp_ids = jnp.arange(dp_count, dtype=jnp.int32)
    same_host = (column_hosts[:, None] == column_hosts[None, :]).astype(jnp.int32)
    host_count = jnp.sum(same_host, axis=1)
    host_place = jnp.sum(same_host * (dp_ids[None, :] < dp_ids[:, None]).astype(jnp.int32), axis=1)
    sources = dp_index * expert_count + jnp.arange(expert_count, dtype=jnp.int32)
    serves = sources[None, :] % host_count[:, None] == host_place[:, None]
    local_of = column_hosts - local_experts * column_index
    kept_mask = serves[:, :, None, None]
    zero_value = jnp.zeros((), jnp.bfloat16)
    picked_input = jnp.where(kept_mask, jnp.take(got_input, local_of, axis=0), zero_value)
    picked_grad = jnp.where(kept_mask, jnp.take(got_grad, local_of, axis=0), zero_value)
    arrived_input, arrived_grad = (
        lax.all_to_all(picked_input, "dp", split_axis=0, concat_axis=0, tiled=True),
        lax.all_to_all(picked_grad, "dp", split_axis=0, concat_axis=0, tiled=True),
    )
    fetched_in, fetched_out = (
        lax.all_gather(adapter_in.astype(jnp.bfloat16), "dp", axis=1, tiled=True),
        lax.all_gather(adapter_out.astype(jnp.bfloat16), "dp", axis=1, tiled=True),
    )
    hosted_local = slot_expert[dp_index, column_index] - local_experts * column_index
    owned_input = lax.dynamic_index_in_dim(fetched_in, hosted_local, 0, keepdims=False)
    own_out = lax.dynamic_index_in_dim(fetched_out, hosted_local, 0, keepdims=False)
    buffer_rows = arrived_input.reshape(buffer_size, width)
    gradient_row_block = arrived_grad.reshape(buffer_size, width)
    gate_weight = frozen_gate[0]
    up_weight = frozen_up[0]
    down_weight = frozen_down[0]
    gate_pre = jnp.dot(buffer_rows, gate_weight, preferred_element_type=jnp.float32)
    up_pre = jnp.dot(buffer_rows, up_weight, preferred_element_type=jnp.float32)
    sigmoid_gate = jax.nn.sigmoid(gate_pre)
    hidden_state = (gate_pre * sigmoid_gate * up_pre).astype(jnp.bfloat16)
    low_rank_input = contract_product(hidden_state, owned_input, 1, 1).astype(jnp.bfloat16)
    low_rank_gradient = contract_product(gradient_row_block, own_out, 1, 1).astype(jnp.bfloat16)
    hidden_gradient = contract_product(gradient_row_block, down_weight, 1, 1)
    hidden_gradient = hidden_gradient + adapter_scale_factor * jnp.dot(
        low_rank_gradient, owned_input, preferred_element_type=jnp.float32
    )
    up_grad = (hidden_gradient * gate_pre * sigmoid_gate).astype(jnp.bfloat16)
    gate_grad = (
        hidden_gradient * up_pre * sigmoid_gate * (1.0 + gate_pre * (1.0 - sigmoid_gate))
    ).astype(jnp.bfloat16)
    back_rows = (
        contract_product(gate_grad, gate_weight, 1, 1) + contract_product(up_grad, up_weight, 1, 1)
    ).astype(jnp.bfloat16)
    incoming_gradient = adapter_scale_factor * contract_product(
        low_rank_gradient, hidden_state, 0, 0
    )
    outgoing_gradient = adapter_scale_factor * contract_product(
        low_rank_input, gradient_row_block, 0, 0
    )
    back_block = back_rows.reshape(dp_count, expert_count, capacity, width)
    came_back = lax.all_to_all(back_block, "dp", split_axis=0, concat_axis=0, tiled=True)
    pieces_back = []
    for which_local in range(local_experts):
        chosen_mask = (serves & (local_of == which_local)[:, None])[:, :, None, None]
        pieces_back.append(jnp.sum(jnp.where(chosen_mask, came_back, zero_value), axis=0))
    gone_back = lax.all_to_all(
        jnp.stack(pieces_back), "expert", split_axis=1, concat_axis=1, tiled=True
    )
    per_row = jnp.take(gone_back.reshape(col_size, width), col_position, axis=0)
    input_grad = jnp.sum(
        per_row.reshape(token_count, top_count, width).astype(jnp.float32), axis=1
    ).astype(jnp.bfloat16)
    selector = (jnp.arange(local_experts, dtype=jnp.int32) == hosted_local).astype(jnp.float32)
    placed_in = selector[:, None, None] * incoming_gradient[None, :, :]
    placed_out = selector[:, None, None] * outgoing_gradient[None, :, :]
    summed_in, summed_out = (
        lax.psum_scatter(placed_in, "dp", scatter_dimension=1, tiled=True),
        lax.psum_scatter(placed_out, "dp", scatter_dimension=1, tiled=True),
    )
    step_in, momentum_in, variance_in = adamw(adapter_in, summed_in, moment_in, second_in)
    step_out, momentum_out, variance_out = adamw(adapter_out, summed_out, moment_out, second_out)
    copied_in, copied_out = (
        lax.all_gather(step_in.astype(jnp.bfloat16), "dp", axis=1, tiled=True),
        lax.all_gather(step_out.astype(jnp.bfloat16), "dp", axis=1, tiled=True),
    )
    replica_in = lax.dynamic_index_in_dim(copied_in, hosted_local, 0, keepdims=True)
    replica_out = lax.dynamic_index_in_dim(copied_out, hosted_local, 0, keepdims=True)
    return (
        input_grad,
        step_in,
        step_out,
        momentum_in,
        momentum_out,
        variance_in,
        variance_out,
        replica_in,
        replica_out,
    )


def flip_chip(array, distance, size):
    return lax.ppermute(array, "expert", [(i, i ^ (2 * distance)) for i in range(size)])


def flip_core(array, size):
    return lax.ppermute(array, "expert", [(i, i ^ 1) for i in range(size)])


def flip_plane(array, dp_count, size, masks):
    pairs = [
        (row * size + col, (row ^ masks[col % 2]) * size + col)
        for row in range(dp_count)
        for col in range(size)
    ]
    return lax.ppermute(array, ("dp", "expert"), pairs)


def add_rounded(left, right):
    return (left.astype(jnp.float32) + right.astype(jnp.float32)).astype(jnp.bfloat16)


def dense_probs(route_probs, expert_choice, expert_total):
    ids = jnp.arange(expert_total, dtype=jnp.int32)
    named = expert_choice[:, :, None] == ids[None, None, :]
    return jnp.sum(jnp.where(named, route_probs[:, :, None], 0.0), axis=1)


def split_three(value):
    high = lax.reduce_precision(value, 8, 7)
    rest = value - high
    middle = lax.reduce_precision(rest, 8, 7)
    low = rest - middle
    return [part.astype(jnp.bfloat16) for part in (high, middle, low)]


def pick_local(stacked, local_of):
    count = stacked.shape[0]
    total = jnp.zeros((local_of.shape[0],) + stacked.shape[1:], stacked.dtype)
    for which in range(count):
        chosen = (local_of == which).reshape((-1,) + (1,) * (stacked.ndim - 1))
        total = jnp.where(chosen, stacked[which][None], total)
    return total


def transposed_dot(left, right):
    return lax.dot_general(
        left, right, (((1,), (1,)), ((), ())), preferred_element_type=jnp.float32
    )


def expert_kernel(sizes, out_sizes, places, chip_ids, token_rows, expert_total, hosts, *refs):
    count = len(sizes)
    pieces, refs = refs[:count], refs[count:]
    gate_w, up_w, down_w, pair = refs[:4]
    backs, refs = refs[4 : 4 + len(out_sizes)], refs[4 + len(out_sizes) :]
    grads, given, grad_rows, hidden_s, gate_g, up_g, served = refs
    dp_index, column_index = lax.axis_index("dp"), lax.axis_index("expert")
    core = lax.rem(column_index, 2)
    hosted = hosts[dp_index, column_index]
    host_count, host_place = jnp.int32(0), jnp.int32(0)
    for row in range(hosts.shape[0]):
        same = (hosts[row, column_index] == hosted).astype(jnp.int32)
        host_count = host_count + same
        host_place = host_place + jnp.where(row < dp_index, same, 0)
    width, hidden = gate_w.shape
    total = given.shape[0]
    coded_width = pieces[0].shape[1] - 2 * width
    column = lax.broadcasted_iota(jnp.int32, (token_rows, coded_width), 1)
    chosen = (lax.rem(column, expert_total) == hosted) & (column < 3 * expert_total)
    for i, (masks, other, chip_id) in enumerate(
        (masks, other, chip_id) for masks, other in places for chip_id in chip_ids
    ):
        row = lax.bitwise_xor(dp_index, jnp.where(core == 0, masks[0], masks[1]))
        source_col = lax.bitwise_xor(column_index, 2 * chip_id + other)
        source = row * hosts.shape[1] + source_col
        served[i] = (lax.rem(source, host_count) == host_place).astype(jnp.int32)
    start = 0
    for piece, size in zip(pieces, sizes):

        def prepare(j, carry, piece=piece, start=start):
            here = pl.ds(pl.multiple_of(j * token_rows, token_rows), token_rows)
            there = pl.ds(pl.multiple_of(start + j * token_rows, token_rows), token_rows)
            coded = piece[here, 2 * width :].astype(jnp.float32)
            prob = jnp.sum(jnp.where(chosen, coded, 0.0), axis=1, keepdims=True)
            prob = jnp.where(served[start // token_rows + j] != 0, prob, 0.0)
            keep = jnp.where(prob != 0, 1.0, 0.0).astype(jnp.bfloat16)
            given[there, :] = piece[here, :width] * keep
            gradient = piece[here, width : 2 * width].astype(jnp.float32)
            grad_rows[there, :] = (prob * gradient).astype(jnp.bfloat16)
            return carry

        lax.fori_loop(0, size // token_rows, prepare, 0)
        start += size
    low_grad = transposed_dot(grad_rows[...], pair[:, hidden:]).astype(jnp.bfloat16)
    tile = 256 if hidden % 256 == 0 else hidden

    def middle(t, low_in):
        cols = pl.ds(pl.multiple_of(t * tile, tile), tile)
        gate = jnp.dot(given[...], gate_w[:, cols], preferred_element_type=jnp.float32)
        up = jnp.dot(given[...], up_w[:, cols], preferred_element_type=jnp.float32)
        sigmoid = jax.nn.sigmoid(gate)
        owned = pair[:, cols]
        state = (gate * sigmoid * up).astype(jnp.bfloat16)
        hidden_s[:, cols] = state
        grad = transposed_dot(grad_rows[...], down_w[cols, :])
        grad = grad + adapter_scale_factor * jnp.dot(
            low_grad, owned, preferred_element_type=jnp.float32
        )
        up_g[:, cols] = (grad * gate * sigmoid).astype(jnp.bfloat16)
        gate_g[:, cols] = (grad * up * sigmoid * (1.0 + gate * (1.0 - sigmoid))).astype(
            jnp.bfloat16
        )
        return low_in + transposed_dot(state, owned)

    low_in = lax.fori_loop(
        0, hidden // tile, middle, jnp.zeros((total, pair.shape[0]), jnp.float32)
    )
    wide = 256 if width % 256 == 0 else width

    def last(t, carry):
        cols = pl.ds(pl.multiple_of(t * wide, wide), wide)
        back = transposed_dot(gate_g[...], gate_w[cols, :]) + transposed_dot(
            up_g[...], up_w[cols, :]
        )
        begin = 0
        for out, size in zip(backs, out_sizes):
            out[:, cols] = back[begin : begin + size].astype(jnp.bfloat16)
            begin += size
        return carry

    lax.fori_loop(0, width // wide, last, 0)
    grads[:, :hidden] = adapter_scale_factor * contract_product(low_grad, hidden_s[...], 0, 0)
    grads[:, hidden:] = adapter_scale_factor * contract_product(
        low_in.astype(jnp.bfloat16), grad_rows[...], 0, 0
    )


def run_rows(
    pieces, out_sizes, places, chip_ids, hosts, weights, pair, token_rows, expert_total
):
    gate, up, down = weights
    width, hidden = gate.shape
    sizes = [piece.shape[0] for piece in pieces]
    total = sum(sizes)
    rank = pair.shape[0]
    local = pl.BlockSpec(memory_space=pltpu.VMEM)
    bf16 = jnp.bfloat16
    out = pl.pallas_call(
        functools.partial(
            expert_kernel, sizes, out_sizes, places, chip_ids, token_rows, expert_total
        ),
        out_shape=[jax.ShapeDtypeStruct((size, width), bf16) for size in out_sizes]
        + [jax.ShapeDtypeStruct((rank, hidden + width), jnp.float32)],
        in_specs=[pl.BlockSpec(memory_space=pltpu.SMEM)] + [local] * (len(pieces) + 4),
        out_specs=[local] * (len(out_sizes) + 1),
        scratch_shapes=[
            pltpu.VMEM((total, width), bf16),
            pltpu.VMEM((total, width), bf16),
            pltpu.VMEM((total, hidden), bf16),
            pltpu.VMEM((total, hidden), bf16),
            pltpu.VMEM((total, hidden), bf16),
            pltpu.SMEM((total // token_rows,), jnp.int32),
        ],
        compiler_params=pltpu.CompilerParams(vmem_limit_bytes=VMEM_LIMIT),
        cost_estimate=pl.CostEstimate(
            flops=2 * total * (5 * width * hidden + 3 * rank * (width + hidden)),
            bytes_accessed=6 * width * hidden + total * 6 * width,
            transcendentals=total * hidden,
        ),
    )(hosts, *pieces, gate, up, down, pair)
    return list(out[:-1]), out[-1]


def z_groups(chips):
    return [[0, 1], list(range(2, chips))]


def dense_device(
    saved_input,
    output_grad,
    route_probs,
    expert_choice,
    slot_expert,
    frozen_gate,
    frozen_up,
    frozen_down,
    adapter_in,
    adapter_out,
    moment_in,
    moment_out,
    second_in,
    second_out,
):
    dp_count = lax.axis_size("dp")
    expert_count = lax.axis_size("expert")
    column_index = lax.axis_index("expert")
    local_experts = adapter_in.shape[0]
    tokens, _ = expert_choice.shape
    width = saved_input.shape[1]
    hidden = adapter_in.shape[2]
    expert_total = local_experts * expert_count
    chips = expert_count // 2
    bf16, f32 = jnp.bfloat16, jnp.float32
    first, second = (1, 2), (2, 1)

    parts = split_three(dense_probs(route_probs, expert_choice, expert_total))
    spare = -(-3 * expert_total // 128) * 128 - 3 * expert_total
    block = jnp.concatenate(
        [saved_input, output_grad, *parts, jnp.zeros((tokens, spare), bf16)], axis=1
    )
    gathered = [block]
    for z in range(1, chips):
        gathered.append(flip_chip(block, z, expert_count))

    hosts = lax.dynamic_index_in_dim(slot_expert, column_index, 1, keepdims=False)
    local_of = hosts - local_experts * column_index
    adapters = jnp.concatenate([adapter_in, adapter_out], axis=2).astype(bf16)
    rank = dp_count * adapter_in.shape[1]
    pair = lax.all_to_all(
        pick_local(adapters, local_of), "dp", split_axis=0, concat_axis=0, tiled=True
    ).reshape(rank, hidden + width)

    weights = (frozen_gate[0], frozen_up[0], frozen_down[0])

    def compute(pieces, out_sizes, places, chip_ids):
        return run_rows(
            pieces, out_sizes, places, chip_ids, slot_expert, weights, pair, tokens, expert_total
        )

    grads = []
    returned = {}

    def rows_of(pieces, out_sizes, places, chip_ids):
        backs, grad = compute(pieces, out_sizes, places, chip_ids)
        grads.append(grad)
        return backs

    own_places = [((0, 0), 0), ((0, 0), 1)]
    side_places = [(first, 0), (first, 1)]
    cross_places = [(second, 1), (second, 0)]
    far_places = [((3, 3), 0), ((3, 3), 1)]
    groups = z_groups(chips)
    for number, chip_ids in enumerate(groups):
        half = len(chip_ids) * tokens
        mine = jnp.concatenate([gathered[z] for z in chip_ids], axis=0)
        if number == 0:
            mine, pair = lax.optimization_barrier((mine, pair))
        other = flip_core(mine, expert_count)
        own = jnp.concatenate([mine, other], axis=0)
        side = flip_plane(own, dp_count, expert_count, first)
        far_mine = flip_plane(side[:half], dp_count, expert_count, second)
        cross = flip_core(side, expert_count)
        far_other = flip_core(far_mine, expert_count)
        if number + 1 < len(groups):
            own_mine, own_other = rows_of([own], [half, half], own_places, chip_ids)
            side_late, side_early, cross_back, far_back, far_away = rows_of(
                [side, cross, far_mine, far_other],
                [half, half, 2 * half, half, half],
                side_places + cross_places + far_places,
                chip_ids,
            )
        else:
            own_mine, own_other, side_late, side_early = rows_of(
                [own, side], [half] * 4, own_places + side_places, chip_ids
            )
            cross_back, far_back, far_away = rows_of(
                [cross, far_mine, far_other],
                [2 * half, half, half],
                cross_places + far_places,
                chip_ids,
            )
        far_got_core = flip_core(far_away, expert_count)
        far_sum = add_rounded(far_back, far_got_core)
        far_got = flip_plane(far_sum, dp_count, expert_count, second)
        cross_got = flip_core(cross_back, expert_count)
        early = add_rounded(side_early, cross_got[half:])
        early_got = flip_plane(early, dp_count, expert_count, first)
        other_sum = add_rounded(own_other, early_got)
        other_got = flip_core(other_sum, expert_count)
        late = (
            side_late.astype(f32) + cross_got[:half].astype(f32) + far_got.astype(f32)
        ).astype(bf16)
        late_got = flip_plane(late, dp_count, expert_count, first)
        total = (own_mine.astype(f32) + other_got.astype(f32) + late_got.astype(f32)).astype(bf16)
        for i, z in enumerate(chip_ids):
            piece = total[i * tokens : (i + 1) * tokens]
            returned[z] = piece if z == 0 else flip_chip(piece, z, expert_count)
    input_grad = sum(piece.astype(f32) for piece in returned.values()).astype(bf16)

    slot_grad = sum(grads).astype(bf16)
    shares = lax.all_to_all(
        slot_grad.reshape(dp_count, rank // dp_count, hidden + width),
        "dp",
        split_axis=0,
        concat_axis=0,
        tiled=True,
    ).astype(f32)
    summed = jnp.stack(
        [
            jnp.sum(jnp.where((local_of == which)[:, None, None], shares, 0.0), axis=0)
            for which in range(local_experts)
        ]
    )
    step_in, momentum_in, variance_in = adamw(
        adapter_in, summed[:, :, :hidden], moment_in, second_in
    )
    step_out, momentum_out, variance_out = adamw(
        adapter_out, summed[:, :, hidden:], moment_out, second_out
    )
    steps = jnp.concatenate([step_in, step_out], axis=2).astype(bf16)
    copied = lax.all_to_all(
        pick_local(steps, local_of), "dp", split_axis=0, concat_axis=0, tiled=True
    ).reshape(1, rank, hidden + width)
    return (
        input_grad,
        step_in,
        step_out,
        momentum_in,
        momentum_out,
        variance_in,
        variance_out,
        copied[:, :, :hidden],
        copied[:, :, hidden:],
    )


def runs_dense(dp_count, expert_count):
    return dp_count == 4 and expert_count == 8


def per_device(saved_input, output_grad, route_probs, expert_choice, *rest):
    dp_count = lax.axis_size("dp")
    expert_count = lax.axis_size("expert")
    tokens, top_count = expert_choice.shape
    local_experts = rest[4].shape[0]
    row_count = tokens * top_count
    capacity = max(2, -(-3 * row_count // (2 * local_experts * expert_count)))
    if tokens <= 2 * capacity and runs_dense(dp_count, expert_count):
        return dense_device(saved_input, output_grad, route_probs, expert_choice, *rest)
    return packed_device(saved_input, output_grad, route_probs, expert_choice, *rest)


def solution(mesh):
    return jax.shard_map(
        per_device,
        mesh=mesh,
        in_specs=(
            P(("dp", "expert"), None),
            P(("dp", "expert"), None),
            P(("dp", "expert"), None),
            P(("dp", "expert"), None),
            P(),
            P(("dp", "expert"), None, None),
            P(("dp", "expert"), None, None),
            P(("dp", "expert"), None, None),
            P("expert", "dp", None),
            P("expert", "dp", None),
            P("expert", "dp", None),
            P("expert", "dp", None),
            P("expert", "dp", None),
            P("expert", "dp", None),
        ),
        out_specs=(
            P(("dp", "expert"), None),
            P("expert", "dp", None),
            P("expert", "dp", None),
            P("expert", "dp", None),
            P("expert", "dp", None),
            P("expert", "dp", None),
            P("expert", "dp", None),
            P(("dp", "expert"), None, None),
            P(("dp", "expert"), None, None),
        ),
        check_vma=False,
    )
```
